32 devices in a mesh: ay: 4 (over x, core), ax: 8 (over z, y).
Axes of the slice: x: 2, y: 2, z: 4, core: 2. Of those that a mesh axis runs over, the one named last changes fastest.
Arguments:
- gaseous_model: float32 [4, 4096, 4096], P(None, 'ay', 'ax'), may hold values from -6 to 6
- forcing_boundary: float32 [4, 4096, 4096], P(None, 'ay', 'ax'), may hold values from -16 to 16, as said below
- relaxation_strength_profile: float32 [4], replicated, may hold values from 0.2 to 1
- bottom_exchange_aloft: bfloat16 [8, 4096, 4096], P(None, 'ay', 'ax'), may hold values from -6 to 6
- exchange_bottom_sensitivity: float32 [8], replicated, may hold values from -1 to 1
- terrain_skin_warmth: bfloat16 [4096, 4096], P('ay', 'ax'), may hold values from -6 to 6
- tile_processor_home: int32 [16384], replicated, may hold values from 0 to 32, as said below
- marine_place_warmth: float32 [16384, 2304], P(('ay', 'ax')), may hold values from -6 to 6
- warming_coefficient: float32 [8], replicated, may hold values from -0.5 to 0.5
Outputs:
- atmosphere_out: float32 [4, 4096, 4096], P(None, 'ay', 'ax')
- ocean_flux: bfloat16 [16384, 8, 2304], P(('ay', 'ax'))
- ocean_sst_out: float32 [16384, 2304], P(('ay', 'ax'))
- surface_temp: float32 [4096, 4096], P('ay', 'ax')
The draws below stay inside these ranges and needn't reach their ends.
Inputs may be any that keep to these rules, and one draw needn't show every extreme that they name: `forcing_boundary`: smooth large-scale patterns with cell-to-cell noise. `tile_processor_home`: 32 marks an all-land block that no ocean device holds. Among the 512 blocks of one tile at most 32 have the same owner, and some tile has exactly 32 with one owner. An ocean device holds at most 512 blocks, and some device holds exactly 512.
All inputs are finite; a program needn't handle non-finite values.
Results may differ from the reference program's by a relative error of at most 0.0037.
Values may be sent and summed in bfloat16 or wider, within the bound.
A program may use at most 192 MiB of HBM per device.

```python
import math
import jax
import jax.numpy as jnp
from jax import lax

GRID = 4096
KMAX = 32
LEVELS = 4
EXCHANGE_KINDS = 8
ABLOCK = 32
MARINE_TILE_EDGE = 48
GAS_PATCH_TOTAL = 1024
MARINE_PATCHES = 2304
BLK_DEV = 512
CAP = 32
UNIT_PLACES = 512
N_AY = 4
N_AX = 8
DEVICES = 32


def wave_table(length, waves_top):
    points = jnp.arange(length, dtype=jnp.int32)
    wavenumbers = jnp.arange(1, waves_top + 1, dtype=jnp.int32)
    phases = points[:, None] * wavenumbers[None, :] % length
    angles = phases.astype(jnp.float32) * (2.0 * math.pi / length)
    constant = jnp.full((length, 1), math.sqrt(1.0 / length), jnp.float32)
    factor = math.sqrt(2.0 / length)
    return jnp.concatenate([constant, factor * jnp.cos(angles), factor * jnp.sin(angles)], axis=1)


def draw_forcing_boundary(key, part):
    key_smooth, key_noise = jax.random.split(jax.random.fold_in(key, 11), 2)
    harmonics = wave_table(GRID, KMAX)
    mode_count = 2 * KMAX + 1
    amplitude = jax.random.normal(key_smooth, (LEVELS, mode_count, mode_count), jnp.float32) * (GRID / mode_count)
    noise_part = 0.5 * jax.random.normal(key_noise, (LEVELS, GRID, GRID), jnp.float32)
    smooth = jnp.einsum('ym,lmn,xn->lyx', harmonics, amplitude, harmonics)
    return jnp.clip(smooth + noise_part, -16.0, 16.0)


def draw_tile_processor_home(key, part):
    key_order, key_shift, key_local, key_land = jax.random.split(jax.random.fold_in(key, 23), 4)
    groups = BLK_DEV // CAP
    owner_order = jax.random.permutation(key_order, DEVICES).astype(jnp.int32)
    group_shift = jax.random.permutation(key_shift, DEVICES).astype(jnp.int32)[:groups]
    device_keys = jax.random.split(key_local, DEVICES)
    shuffled = jax.vmap(lambda single: jax.random.permutation(single, BLK_DEV))(device_keys).astype(jnp.int32)
    group_of = shuffled // CAP
    source = jnp.arange(DEVICES, dtype=jnp.int32)[:, None]
    owner_rank = (source + group_shift[group_of]) % DEVICES
    owner_of = owner_order[owner_rank]
    land_level = owner_rank * 4 // DEVICES
    land_draw = jax.random.randint(key_land, (DEVICES, BLK_DEV), 0, 8, jnp.int32)
    is_wet = land_draw >= land_level
    return jnp.where(is_wet, owner_of, DEVICES).reshape(-1).astype(jnp.int32)


def block_scale(stream_key, extent, pieces, smallest, top_value):
    gain, own = 1.0, jax.random.fold_in(stream_key, 6)
    for dim, blocks in pieces:
        draws = jnp.exp(jax.random.uniform(jax.random.fold_in(own, dim), (blocks,), jnp.float32, smallest / len(pieces), top_value / len(pieces)))
        gain = gain * jnp.repeat(draws, extent[dim] // blocks).reshape([-1 if axis == dim else 1 for axis in range(len(extent))])
    return gain


def normal_values(own_key, dims, width, limit, cuts=(), kind=jnp.bfloat16):
    level = block_scale(own_key, dims, cuts, -0.22, 0.18) if cuts else 1.0
    entries = jax.random.normal(own_key, dims, jnp.float32) * width * level
    return jnp.minimum(jnp.maximum(entries, -limit), limit).astype(kind)


def setup_inputs(seed: int = 0) -> dict:
    arg_keys = jax.random.split(jax.random.key(seed), 10)
    gaseous_model = normal_values(arg_keys[0], (LEVELS, GRID, GRID), 1.0, 6.0, ((1, 4), (2, 8)), jnp.float32)
    forcing_boundary = draw_forcing_boundary(jax.random.fold_in(arg_keys[9], 71), 0)
    relaxation_strength_profile = jnp.clip(jnp.exp(jax.random.uniform(arg_keys[2], (LEVELS,), jnp.float32, math.log(0.2), math.log(1.0))), 0.2, 1.0)
    bottom_exchange_aloft = normal_values(arg_keys[3], (EXCHANGE_KINDS, GRID, GRID), 1.0, 6.0, ((1, 4), (2, 8)))
    exchange_bottom_sensitivity = jnp.clip(jax.random.uniform(arg_keys[4], (EXCHANGE_KINDS,), jnp.float32, -1.0, 1.0), -1.0, 1.0)
    terrain_skin_warmth = normal_values(arg_keys[5], (GRID, GRID), 1.0, 6.0, ((0, 4), (1, 8)))
    tile_processor_home = draw_tile_processor_home(jax.random.fold_in(arg_keys[9], 71), 0)
    marine_place_warmth = normal_values(arg_keys[7], (DEVICES * UNIT_PLACES, MARINE_PATCHES), 1.0, 6.0, ((0, 32),), jnp.float32)
    warming_coefficient = jnp.clip(jax.random.uniform(arg_keys[8], (EXCHANGE_KINDS,), jnp.float32, -0.5, 0.5), -0.5, 0.5)
    return dict(gaseous_model=gaseous_model, forcing_boundary=forcing_boundary, relaxation_strength_profile=relaxation_strength_profile, bottom_exchange_aloft=bottom_exchange_aloft, exchange_bottom_sensitivity=exchange_bottom_sensitivity, terrain_skin_warmth=terrain_skin_warmth, tile_processor_home=tile_processor_home, marine_place_warmth=marine_place_warmth, warming_coefficient=warming_coefficient)


highest_accuracy = lax.Precision.HIGHEST

def spectral_basis(length, offset, number, waves_top):
    points = offset + jnp.arange(number, dtype=jnp.int32)
    wavenumbers = jnp.arange(1, waves_top + 1, dtype=jnp.int32)
    phases = points[:, None] * wavenumbers[None, :] % length
    angles = phases.astype(jnp.float32) * (2.0 * math.pi / length)
    constant = jnp.full((number, 1), math.sqrt(1.0 / length), jnp.float32)
    factor = math.sqrt(2.0 / length)
    return jnp.concatenate([constant, factor * jnp.cos(angles), factor * jnp.sin(angles)], axis=1)

def intersection_table():
    ocean_index = jnp.arange(MARINE_TILE_EDGE, dtype=jnp.int32)[:, None]
    air_index = jnp.arange(ABLOCK, dtype=jnp.int32)[None, :]
    upper_edge = jnp.minimum(2 * ocean_index + 2, 3 * air_index + 3)
    lower_edge = jnp.maximum(2 * ocean_index, 3 * air_index)
    return jnp.maximum(upper_edge - lower_edge, 0).astype(jnp.float32)

def reference(gaseous_model, forcing_boundary, relaxation_strength_profile, bottom_exchange_aloft, exchange_bottom_sensitivity, terrain_skin_warmth, tile_processor_home, marine_place_warmth, warming_coefficient):
    harmonics = spectral_basis(GRID, 0, GRID, KMAX)
    departure = forcing_boundary - gaseous_model
    along_cols = jnp.einsum('lyx,xn->lyn', departure, harmonics, precision=highest_accuracy)
    coefficients = jnp.einsum('ym,lyn->lmn', harmonics, along_cols, precision=highest_accuracy)
    rows_back = jnp.einsum('ym,lmn->lyn', harmonics, coefficients, precision=highest_accuracy)
    filtered = jnp.einsum('lyn,xn->lyx', rows_back, harmonics, precision=highest_accuracy)
    advanced_condition = gaseous_model + relaxation_strength_profile[:, None, None] * filtered
    flux_air = (bottom_exchange_aloft.astype(jnp.float32) + exchange_bottom_sensitivity[:, None, None] * advanced_condition[LEVELS - 1]).astype(jnp.bfloat16)
    tile_rows = GRID // N_AY
    tile_cols = GRID // N_AX
    block_rows = tile_rows // ABLOCK
    block_cols = tile_cols // ABLOCK
    processor_portion = block_rows * block_cols
    processor_roster = N_AY * N_AX
    block_total = processor_roster * processor_portion
    blocks = flux_air.reshape(EXCHANGE_KINDS, N_AY, block_rows, ABLOCK, N_AX, block_cols, ABLOCK)
    blocks = blocks.transpose(1, 4, 2, 5, 0, 3, 6).reshape(block_total, EXCHANGE_KINDS, ABLOCK, ABLOCK)
    is_wet = tile_processor_home < processor_roster
    one_hot = (tile_processor_home[:, None] == jnp.arange(processor_roster + 1, dtype=jnp.int32)[None, :]).astype(jnp.int32)
    ranking = lax.optimization_barrier(jnp.sum((jnp.cumsum(one_hot, axis=0) - one_hot) * one_hot, axis=1)).astype(jnp.int32)
    numbers = jnp.arange(block_total, dtype=jnp.int32)
    slot_index = jnp.where(is_wet, tile_processor_home * processor_portion + ranking, processor_roster * processor_portion).astype(jnp.int32)
    place_tile_position = jnp.full((processor_roster * processor_portion,), block_total, jnp.int32).at[slot_index].set(numbers, mode='drop')
    forward_weights = intersection_table() / 2.0
    backward_coefficients = intersection_table() / 3.0

    def marine_labour(given_tensors):
        picked_option, marine_warmth_lines = given_tensors
        possessed_indicator = picked_option < block_total
        picked = blocks[jnp.minimum(picked_option, block_total - 1)].astype(jnp.float32)
        regrid = jnp.einsum('oa,sfac,pc->sfop', forward_weights, picked, forward_weights, precision=highest_accuracy)
        marine_exchange_mesh = jnp.where(possessed_indicator[:, None, None, None], regrid, 0.0).astype(jnp.bfloat16)
        marine_exchange_mesh = marine_exchange_mesh.reshape(processor_portion, EXCHANGE_KINDS, MARINE_PATCHES)
        marine_warming = jnp.einsum('f,sfk->sk', warming_coefficient, marine_exchange_mesh.astype(jnp.float32), precision=highest_accuracy)
        renewed_marine_warmth = jnp.where(possessed_indicator[:, None], marine_warmth_lines + marine_warming, 0.0)
        sent_back_entries = jnp.einsum('en,oea,am->onm', backward_coefficients, renewed_marine_warmth.reshape(processor_portion, MARINE_TILE_EDGE, MARINE_TILE_EDGE), backward_coefficients, precision=highest_accuracy)
        return (marine_exchange_mesh, renewed_marine_warmth, sent_back_entries.reshape(processor_portion, GAS_PATCH_TOTAL))
    exchange_outcome, marine_warmth_product, sent_back_entries = lax.map(marine_labour, (place_tile_position.reshape(processor_roster, processor_portion), marine_place_warmth.reshape(processor_roster, processor_portion, MARINE_PATCHES)))
    returned_flat = sent_back_entries.reshape(processor_roster * processor_portion, GAS_PATCH_TOTAL)
    position = jnp.where(is_wet, tile_processor_home * processor_portion + ranking, 0).astype(jnp.int32)
    air_blocks = returned_flat[position]
    land_blocks = terrain_skin_warmth.reshape(N_AY, block_rows, ABLOCK, N_AX, block_cols, ABLOCK)
    land_blocks = land_blocks.transpose(0, 3, 1, 4, 2, 5).reshape(block_total, GAS_PATCH_TOTAL).astype(jnp.float32)
    surface_blocks = jnp.where(is_wet[:, None], air_blocks, land_blocks)
    bottom_quantity = surface_blocks.reshape(N_AY, N_AX, block_rows, block_cols, ABLOCK, ABLOCK)
    bottom_quantity = bottom_quantity.transpose(0, 2, 4, 1, 3, 5).reshape(GRID, GRID)
    return (advanced_condition, exchange_outcome.reshape(processor_roster * processor_portion, EXCHANGE_KINDS, MARINE_PATCHES), marine_warmth_product.reshape(processor_roster * processor_portion, MARINE_PATCHES), bottom_quantity)
```

```python
import functools
import math

import jax
import jax.numpy as jnp
from jax import lax
from jax.experimental import pallas as pl
from jax.experimental.pallas import tpu as pltpu
from jax.sharding import PartitionSpec as P

GRID = 4096
KMAX = 32
EXCHANGE_KINDS = 8
ABLOCK = 32
MARINE_TILE_EDGE = 48
GAS_PATCH_TOTAL = 1024
MARINE_PATCHES = 2304
LANES = 128
QUAD = LANES // ABLOCK
SLOTS_STEP = 32


highest_accuracy = lax.Precision.HIGHEST


def spectral_basis(length, offset, number, waves_top):
    points = offset + jnp.arange(number, dtype=jnp.int32)
    wavenumbers = jnp.arange(1, waves_top + 1, dtype=jnp.int32)
    phases = points[:, None] * wavenumbers[None, :] % length
    angles = phases.astype(jnp.float32) * (2.0 * math.pi / length)
    constant = jnp.full((number, 1), math.sqrt(1.0 / length), jnp.float32)
    factor = math.sqrt(2.0 / length)
    return jnp.concatenate([constant, factor * jnp.cos(angles), factor * jnp.sin(angles)], axis=1)


def intersection_table():
    ocean_index = jnp.arange(MARINE_TILE_EDGE, dtype=jnp.int32)[:, None]
    air_index = jnp.arange(ABLOCK, dtype=jnp.int32)[None, :]
    upper_edge = jnp.minimum(2 * ocean_index + 2, 3 * air_index + 3)
    lower_edge = jnp.maximum(2 * ocean_index, 3 * air_index)
    return jnp.maximum(upper_edge - lower_edge, 0).astype(jnp.float32)


def sum_kernel(axes, in_ref, out_ref, held, recv, send_sem, recv_sem):
    me = {name: lax.axis_index(name) for name, _ in axes}
    partners = []
    for name, size in axes:
        reach = 1
        while reach < size:
            sign = 1 - 2 * ((me[name] // reach) % 2)
            coords = dict(me)
            coords[name] = me[name] + sign * reach
            partners.append(tuple(coords[axis] for axis, _ in axes))
            reach *= 2
    barrier = pltpu.get_barrier_semaphore()
    for partner in partners:
        pl.semaphore_signal(
            barrier, inc=1, device_id=partner, device_id_type=pl.DeviceIdType.MESH
        )
    pl.semaphore_wait(barrier, len(partners))
    for step, partner in enumerate(partners):
        source = in_ref if step == 0 else held.at[step]
        copy = pltpu.make_async_remote_copy(
            src_ref=source,
            dst_ref=recv.at[step],
            send_sem=send_sem.at[step],
            recv_sem=recv_sem.at[step],
            device_id=partner,
            device_id_type=pl.DeviceIdType.MESH,
        )
        copy.start()
        copy.wait()
        total = source[...] + recv[step]
        if step + 1 < len(partners):
            held[step + 1] = total
        else:
            out_ref[...] = total


def sum_everywhere(partial, axes):
    steps = sum((size - 1).bit_length() for _, size in axes)
    return pl.pallas_call(
        functools.partial(sum_kernel, axes),
        out_shape=jax.ShapeDtypeStruct(partial.shape, partial.dtype),
        in_specs=[pl.BlockSpec(memory_space=pltpu.VMEM)],
        out_specs=pl.BlockSpec(memory_space=pltpu.VMEM),
        scratch_shapes=[
            pltpu.VMEM((steps,) + partial.shape, partial.dtype),
            pltpu.VMEM((steps,) + partial.shape, partial.dtype),
            pltpu.SemaphoreType.DMA((steps,)),
            pltpu.SemaphoreType.DMA((steps,)),
        ],
        compiler_params=pltpu.CompilerParams(collective_id=0, has_side_effects=True),
    )(partial)


def swap_groups(parts):
    group = lax.broadcasted_iota(jnp.int32, parts[0].shape, 1) // ABLOCK
    even = group % 2 == 0
    low = group < 2
    p0, p1, p2, p3 = parts
    a0 = jnp.where(even, p0, pltpu.roll(p1, ABLOCK, 1))
    a1 = jnp.where(even, pltpu.roll(p0, LANES - ABLOCK, 1), p1)
    a2 = jnp.where(even, p2, pltpu.roll(p3, ABLOCK, 1))
    a3 = jnp.where(even, pltpu.roll(p2, LANES - ABLOCK, 1), p3)
    b0 = jnp.where(low, a0, pltpu.roll(a2, 2 * ABLOCK, 1))
    b2 = jnp.where(low, pltpu.roll(a0, 2 * ABLOCK, 1), a2)
    b1 = jnp.where(low, a1, pltpu.roll(a3, 2 * ABLOCK, 1))
    b3 = jnp.where(low, pltpu.roll(a1, 2 * ABLOCK, 1), a3)
    return [b0, b1, b2, b3]


def pack_kernel(block_cols, spill, target, sens, air, aloft, send, stage, sems):
    step = pl.program_id(0)
    last = pl.num_programs(0) - 1
    slot = step % 2

    def copy(row, place, col):
        return pltpu.make_async_copy(
            stage.at[place, col], send.at[target[row * block_cols + col]], sems.at[place, col]
        )

    def each(row, place, start):
        for col in range(block_cols):

            @pl.when(target[row * block_cols + col] < spill)
            def _():
                if start:
                    copy(row, place, col).start()
                else:
                    copy(row, place, col).wait()

    @pl.when(step >= 2)
    def _():
        each(step - 2, slot, False)

    level = air[0]
    fields = []
    for field in range(EXCHANGE_KINDS):
        flux = aloft[field].astype(jnp.float32) + sens[field] * level
        fields.append(flux)
    stacked = jnp.stack(fields, axis=0)
    rows = jnp.swapaxes(stacked, 0, 1)
    tall = ABLOCK // QUAD
    rows = rows.reshape(tall, QUAD, EXCHANGE_KINDS, rows.shape[-1])
    for group in range(block_cols // QUAD):
        parts = [
            rows[:, k, :, group * LANES : (group + 1) * LANES].reshape(tall * EXCHANGE_KINDS, LANES)
            for k in range(QUAD)
        ]
        swapped = swap_groups(parts)
        for j in range(QUAD):
            piece = swapped[j].reshape(tall, EXCHANGE_KINDS, LANES)
            flat = jnp.concatenate([piece[i] for i in range(tall)], axis=1)
            stage[slot, group * QUAD + j] = flat.astype(jnp.bfloat16)
    each(step, slot, True)

    @pl.when(step == last)
    def _():
        @pl.when(last >= 1)
        def _():
            each(step - 1, 1 - slot, False)

        each(step, slot, False)


def pack(advanced, aloft, sens, target, slots):
    levels, tile_rows, tile_cols = advanced.shape
    block_cols = tile_cols // ABLOCK
    return pl.pallas_call(
        functools.partial(pack_kernel, block_cols, slots),
        out_shape=jax.ShapeDtypeStruct((slots, EXCHANGE_KINDS, GAS_PATCH_TOTAL), jnp.bfloat16),
        grid_spec=pltpu.PrefetchScalarGridSpec(
            num_scalar_prefetch=2,
            grid=(tile_rows // ABLOCK,),
            in_specs=[
                pl.BlockSpec((1, ABLOCK, tile_cols), lambda i, *_: (levels - 1, i, 0)),
                pl.BlockSpec((EXCHANGE_KINDS, ABLOCK, tile_cols), lambda i, *_: (0, i, 0)),
            ],
            out_specs=pl.BlockSpec(memory_space=pl.ANY),
            scratch_shapes=[
                pltpu.VMEM((2, block_cols, EXCHANGE_KINDS, GAS_PATCH_TOTAL), jnp.bfloat16),
                pltpu.SemaphoreType.DMA((2, block_cols)),
            ],
        ),
        compiler_params=pltpu.CompilerParams(dimension_semantics=("arbitrary",)),
    )(target, sens, advanced, aloft)


def ocean_kernel(
    batch, arrival, total, incoming, warmth, forward, back, mix, flux_out, sst_out, back_out,
    taken, shaped, stage, in_sems, out_sems,
):
    step = pl.program_id(0)
    last = pl.num_programs(0) - 1
    slot = step % 2

    def fetch(at, place, start):
        for i in range(batch):
            place_of = at * batch + i

            @pl.when(place_of < total[0])
            def _():
                copy = pltpu.make_async_copy(
                    incoming.at[arrival[place_of]], taken.at[place, i], in_sems.at[place, i]
                )
                if start:
                    copy.start()
                else:
                    copy.wait()

    def put(at, place, start):
        for i in range(batch):
            place_of = at * batch + i

            @pl.when(place_of < total[0])
            def _():
                copy = pltpu.make_async_copy(
                    stage.at[place, i], back_out.at[arrival[place_of]], out_sems.at[place, i]
                )
                if start:
                    copy.start()
                else:
                    copy.wait()

    @pl.when(step == 0)
    def _():
        fetch(step, slot, True)

    @pl.when(step < last)
    def _():
        fetch(step + 1, 1 - slot, True)

    fetch(step, slot, False)

    @pl.when(step >= 2)
    def _():
        put(step - 2, slot, False)

    flat = batch * EXCHANGE_KINDS
    air = taken[slot].astype(jnp.float32).reshape(flat, GAS_PATCH_TOTAL)
    row_of = lax.broadcasted_iota(jnp.int32, (flat, 1), 0) // EXCHANGE_KINDS + step * batch
    held_wide = row_of < total[0]
    place = lax.broadcasted_iota(jnp.int32, (batch, 1), 0) + step * batch
    held = place < total[0]
    air_half = GAS_PATCH_TOTAL // 2
    sea_half = MARINE_PATCHES // 2
    for half in range(2):
        sea = slice(half * sea_half, (half + 1) * sea_half)
        part = air[:, half * air_half : (half + 1) * air_half].astype(jnp.bfloat16)
        grid_flux = jnp.dot(part, forward[...], preferred_element_type=jnp.float32)
        grid_flux = jnp.where(held_wide, grid_flux, 0.0).astype(jnp.bfloat16)
        flux_out[:, :, sea] = (
            grid_flux.astype(jnp.float32)
            .reshape(batch, EXCHANGE_KINDS, sea_half)
            .astype(jnp.bfloat16)
        )
        warming = jnp.dot(mix[0], grid_flux, preferred_element_type=jnp.float32)
        warming += jnp.dot(mix[1], grid_flux, preferred_element_type=jnp.float32)
        renewed = jnp.where(held, warmth[:, sea] + warming, 0.0)
        sst_out[:, sea] = renewed
        upper = renewed.astype(jnp.bfloat16)
        lower = (renewed - upper.astype(jnp.float32)).astype(jnp.bfloat16)
        home = jnp.dot(upper, back[...], preferred_element_type=jnp.float32)
        home += jnp.dot(lower, back[...], preferred_element_type=jnp.float32)
        home = home * (1.0 / 9.0)
        pieces = air_half // LANES
        for j in range(pieces):
            shaped[:, half * pieces + j, :] = home[:, j * LANES : (j + 1) * LANES]
    stage[slot] = shaped[...].astype(jnp.bfloat16)
    put(step, slot, True)

    @pl.when(step == last)
    def _():
        @pl.when(last >= 1)
        def _():
            put(step - 1, 1 - slot, False)

        put(step, slot, False)


def ocean(incoming, warmth, arrival, total, forward, back, mix):
    slots = incoming.shape[0]
    portion = warmth.shape[0]
    batch = SLOTS_STEP
    tall = GAS_PATCH_TOTAL // LANES
    return pl.pallas_call(
        functools.partial(ocean_kernel, batch),
        out_shape=(
            jax.ShapeDtypeStruct((portion, EXCHANGE_KINDS, MARINE_PATCHES), jnp.bfloat16),
            jax.ShapeDtypeStruct((portion, MARINE_PATCHES), jnp.float32),
            jax.ShapeDtypeStruct((slots, tall, LANES), jnp.bfloat16),
        ),
        grid_spec=pltpu.PrefetchScalarGridSpec(
            num_scalar_prefetch=2,
            grid=(portion // batch,),
            in_specs=[
                pl.BlockSpec(memory_space=pl.ANY),
                pl.BlockSpec((batch, MARINE_PATCHES), lambda i, *_: (i, 0)),
                pl.BlockSpec(memory_space=pltpu.VMEM),
                pl.BlockSpec(memory_space=pltpu.VMEM),
                pl.BlockSpec(memory_space=pltpu.VMEM),
            ],
            out_specs=(
                pl.BlockSpec((batch, EXCHANGE_KINDS, MARINE_PATCHES), lambda i, *_: (i, 0, 0)),
                pl.BlockSpec((batch, MARINE_PATCHES), lambda i, *_: (i, 0)),
                pl.BlockSpec(memory_space=pl.ANY),
            ),
            scratch_shapes=[
                pltpu.VMEM((2, batch, EXCHANGE_KINDS, GAS_PATCH_TOTAL), jnp.bfloat16),
                pltpu.VMEM((batch, tall, LANES), jnp.float32),
                pltpu.VMEM((2, batch, tall, LANES), jnp.bfloat16),
                pltpu.SemaphoreType.DMA((2, batch)),
                pltpu.SemaphoreType.DMA((2, batch)),
            ],
        ),
        compiler_params=pltpu.CompilerParams(
            dimension_semantics=("arbitrary",), vmem_limit_bytes=48 * 1024 * 1024
        ),
    )(arrival, total, incoming, warmth, forward, back, mix)


def surface_kernel(block_cols, spill, target, home, land, wet, out, taken, merged, sems):
    step = pl.program_id(0)
    last = pl.num_programs(0) - 1
    slot = step % 2

    def fetch(row, place, start):
        for col in range(block_cols):

            @pl.when(target[row * block_cols + col] < spill)
            def _():
                copy = pltpu.make_async_copy(
                    home.at[target[row * block_cols + col]],
                    taken.at[place, col],
                    sems.at[place, col],
                )
                if start:
                    copy.start()
                else:
                    copy.wait()

    @pl.when(step == 0)
    def _():
        fetch(step, slot, True)

    @pl.when(step < last)
    def _():
        fetch(step + 1, 1 - slot, True)

    fetch(step, slot, False)
    tall = ABLOCK // QUAD
    for group in range(block_cols // QUAD):
        parts = [taken[slot, group * QUAD + j].astype(jnp.float32) for j in range(QUAD)]
        lines = swap_groups(parts)
        for k in range(QUAD):
            merged[group, pl.ds(k, tall, stride=QUAD), :] = lines[k]
        span = slice(group * LANES, (group + 1) * LANES)
        out[:, span] = jnp.where(
            wet[0, :, span] > 0.0, merged[group], land[:, span].astype(jnp.float32)
        )


def surface(home, land, wet_lanes, target):
    tile_rows, tile_cols = land.shape
    block_cols = tile_cols // ABLOCK
    slots, tall, _ = home.shape
    return pl.pallas_call(
        functools.partial(surface_kernel, block_cols, slots),
        out_shape=jax.ShapeDtypeStruct((tile_rows, tile_cols), jnp.float32),
        grid_spec=pltpu.PrefetchScalarGridSpec(
            num_scalar_prefetch=1,
            grid=(tile_rows // ABLOCK,),
            in_specs=[
                pl.BlockSpec(memory_space=pl.ANY),
                pl.BlockSpec((ABLOCK, tile_cols), lambda i, *_: (i, 0)),
                pl.BlockSpec((1, 1, tile_cols), lambda i, *_: (i, 0, 0)),
            ],
            out_specs=pl.BlockSpec((ABLOCK, tile_cols), lambda i, *_: (i, 0)),
            scratch_shapes=[
                pltpu.VMEM((2, block_cols, tall, LANES), jnp.bfloat16),
                pltpu.VMEM((tile_cols // LANES, ABLOCK, LANES), jnp.float32),
                pltpu.SemaphoreType.DMA((2, block_cols)),
            ],
        ),
        compiler_params=pltpu.CompilerParams(dimension_semantics=("arbitrary",)),
    )(target, home, land, wet_lanes)


def body(
    gaseous_model,
    forcing_boundary,
    relaxation_strength_profile,
    bottom_exchange_aloft,
    exchange_bottom_sensitivity,
    terrain_skin_warmth,
    tile_processor_home,
    marine_place_warmth,
    warming_coefficient,
):
    rows_ay = lax.axis_size("ay")
    cols_ax = lax.axis_size("ax")
    processor_roster = rows_ay * cols_ax
    device_id = lax.axis_index("ay") * cols_ax + lax.axis_index("ax")
    _, tile_rows, tile_cols = gaseous_model.shape
    block_rows = tile_rows // ABLOCK
    block_cols = tile_cols // ABLOCK
    processor_portion = block_rows * block_cols
    capacity = 2 * processor_portion // processor_roster
    slots = processor_roster * capacity
    basis_rows = spectral_basis(GRID, lax.axis_index("ay") * tile_rows, tile_rows, KMAX)
    basis_cols = spectral_basis(GRID, lax.axis_index("ax") * tile_cols, tile_cols, KMAX)
    departure = forcing_boundary - gaseous_model
    along_cols = jnp.einsum("lyx,xn->lyn", departure, basis_cols, precision=highest_accuracy)
    partial_sum = jnp.einsum("ym,lyn->lmn", basis_rows, along_cols, precision=highest_accuracy)
    modes = basis_rows.shape[1]
    padding = ((0, 0), (0, -modes % 8), (0, -modes % LANES))
    summed = sum_everywhere(jnp.pad(partial_sum, padding), (("ay", rows_ay), ("ax", cols_ax)))
    coefficients = summed[:, :modes, :modes]
    rows_back = jnp.einsum("ym,lmn->lyn", basis_rows, coefficients, precision=highest_accuracy)
    filtered = jnp.einsum("lyn,xn->lyx", rows_back, basis_cols, precision=highest_accuracy)
    advanced_condition = gaseous_model + relaxation_strength_profile[:, None, None] * filtered

    owners = tile_processor_home.reshape(processor_roster, processor_portion)
    own_owner = lax.dynamic_index_in_dim(owners, device_id, 0, keepdims=False)
    numbers = jnp.arange(processor_portion, dtype=jnp.int32)
    earlier = numbers[:, None] > numbers[None, :]
    matching = own_owner[:, None] == own_owner[None, :]
    own_within = jnp.sum(matching & earlier, axis=1, dtype=jnp.int32)
    is_wet = own_owner < processor_roster
    target = jnp.where(is_wet, own_owner * capacity + own_within, slots).astype(jnp.int32)
    counts = jnp.sum(owners == device_id, axis=1, dtype=jnp.int32)
    tiles = jnp.arange(processor_roster, dtype=jnp.int32)
    ends = jnp.sum(jnp.where(tiles[:, None] >= tiles[None, :], counts[None, :], 0), axis=1)
    passed = numbers[:, None] >= ends[None, :]
    tile_of = jnp.sum(passed, axis=1, dtype=jnp.int32)
    before = jnp.sum(jnp.where(passed, counts[None, :], 0), axis=1, dtype=jnp.int32)
    held_total = jnp.sum(counts, dtype=jnp.int32).reshape(1)
    arrival = jnp.where(numbers < held_total, tile_of * capacity + numbers - before, 0)
    arrival = arrival.astype(jnp.int32)

    table = intersection_table()
    half_table = table[: MARINE_TILE_EDGE // 2, : ABLOCK // 2]
    paired = half_table[:, None, :, None] * table[None, :, None, :]
    paired = paired.reshape(MARINE_PATCHES // 2, GAS_PATCH_TOTAL // 2)
    forward_matrix = (paired / 4.0).T.astype(jnp.bfloat16)
    return_matrix = paired.astype(jnp.bfloat16)
    row_block = jnp.arange(SLOTS_STEP * EXCHANGE_KINDS, dtype=jnp.int32) // EXCHANGE_KINDS
    same = row_block[None, :] == jnp.arange(SLOTS_STEP, dtype=jnp.int32)[:, None]
    weights = jnp.where(same, jnp.tile(warming_coefficient, SLOTS_STEP)[None, :], 0.0)
    upper = lax.reduce_precision(weights, 8, 7)
    mix = jnp.stack([upper, weights - upper]).astype(jnp.bfloat16)
    wet_lanes = jnp.repeat(is_wet.reshape(block_rows, 1, block_cols), ABLOCK, axis=2)

    outgoing = pack(
        advanced_condition, bottom_exchange_aloft, exchange_bottom_sensitivity, target, slots
    )
    incoming = lax.all_to_all(outgoing, ("ay", "ax"), split_axis=0, concat_axis=0, tiled=True)
    marine_exchange_mesh, renewed_marine_warmth, outgoing_back = ocean(
        incoming, marine_place_warmth, arrival, held_total, forward_matrix, return_matrix, mix
    )
    home_rows = lax.all_to_all(outgoing_back, ("ay", "ax"), split_axis=0, concat_axis=0, tiled=True)
    bottom_quantity = surface(
        home_rows, terrain_skin_warmth, wet_lanes.astype(jnp.float32), target
    )
    return (advanced_condition, marine_exchange_mesh, renewed_marine_warmth, bottom_quantity)


def solution(mesh):
    return jax.shard_map(
        body,
        mesh=mesh,
        in_specs=(
            P(None, "ay", "ax"),
            P(None, "ay", "ax"),
            P(),
            P(None, "ay", "ax"),
            P(),
            P("ay", "ax"),
            P(),
            P(("ay", "ax"), None),
            P(),
        ),
        out_specs=(
            P(None, "ay", "ax"),
            P(("ay", "ax"), None, None),
            P(("ay", "ax"), None),
            P("ay", "ax"),
        ),
        check_vma=False,
    )
```

```python
import functools
import math

import jax
import jax.numpy as jnp
from jax import lax
from jax.experimental import pallas as pl
from jax.experimental.pallas import tpu as pltpu
from jax.sharding import PartitionSpec as P

GRID = 4096
KMAX = 32
EXCHANGE_KINDS = 8
ABLOCK = 32
MARINE_TILE_EDGE = 48
GAS_PATCH_TOTAL = 1024
MARINE_PATCHES = 2304
LANES = 128
QUAD = LANES // ABLOCK
SLOTS_STEP = 64
AHEAD = 4


highest_accuracy = lax.Precision.HIGHEST


def spectral_basis(length, offset, number, waves_top):
    points = offset + jnp.arange(number, dtype=jnp.int32)
    wavenumbers = jnp.arange(1, waves_top + 1, dtype=jnp.int32)
    phases = points[:, None] * wavenumbers[None, :] % length
    angles = phases.astype(jnp.float32) * (2.0 * math.pi / length)
    constant = jnp.full((number, 1), math.sqrt(1.0 / length), jnp.float32)
    factor = math.sqrt(2.0 / length)
    return jnp.concatenate([constant, factor * jnp.cos(angles), factor * jnp.sin(angles)], axis=1)


def intersection_table():
    ocean_index = jnp.arange(MARINE_TILE_EDGE, dtype=jnp.int32)[:, None]
    air_index = jnp.arange(ABLOCK, dtype=jnp.int32)[None, :]
    upper_edge = jnp.minimum(2 * ocean_index + 2, 3 * air_index + 3)
    lower_edge = jnp.maximum(2 * ocean_index, 3 * air_index)
    return jnp.maximum(upper_edge - lower_edge, 0).astype(jnp.float32)


def sum_kernel(axes, in_ref, out_ref, held, recv, send_sem, recv_sem):
    me = {name: lax.axis_index(name) for name, _ in axes}
    partners = []
    for name, size in axes:
        reach = 1
        while reach < size:
            sign = 1 - 2 * ((me[name] // reach) % 2)
            coords = dict(me)
            coords[name] = me[name] + sign * reach
            partners.append(tuple(coords[axis] for axis, _ in axes))
            reach *= 2
    barrier = pltpu.get_barrier_semaphore()
    for partner in partners:
        pl.semaphore_signal(
            barrier, inc=1, device_id=partner, device_id_type=pl.DeviceIdType.MESH
        )
    pl.semaphore_wait(barrier, len(partners))
    half = in_ref.shape[0] // 2
    side = me[axes[0][0]] % 2
    own = pl.ds(side * half, half)
    other = pl.ds((1 - side) * half, half)

    def exchange(step, source, landing, partner):
        copy = pltpu.make_async_remote_copy(
            src_ref=source,
            dst_ref=landing,
            send_sem=send_sem.at[step],
            recv_sem=recv_sem.at[step],
            device_id=partner,
            device_id_type=pl.DeviceIdType.MESH,
        )
        copy.start()
        copy.wait()

    exchange(0, in_ref.at[other], recv.at[0], partners[0])
    held[0] = in_ref[own] + recv[0]
    last = len(partners)
    for step in range(1, last):
        exchange(step, held.at[step - 1], recv.at[step], partners[step])
        held[step] = held[step - 1] + recv[step]
    exchange(last, held.at[last - 1], recv.at[last], partners[0])
    out_ref[own] = held[last - 1]
    out_ref[other] = recv[last]


def sum_everywhere(partial, axes):
    steps = sum((size - 1).bit_length() for _, size in axes) + 1
    half = (partial.shape[0] // 2,) + partial.shape[1:]
    return pl.pallas_call(
        functools.partial(sum_kernel, axes),
        out_shape=jax.ShapeDtypeStruct(partial.shape, partial.dtype),
        in_specs=[pl.BlockSpec(memory_space=pltpu.VMEM)],
        out_specs=pl.BlockSpec(memory_space=pltpu.VMEM),
        scratch_shapes=[
            pltpu.VMEM((steps,) + half, partial.dtype),
            pltpu.VMEM((steps,) + half, partial.dtype),
            pltpu.SemaphoreType.DMA((steps,)),
            pltpu.SemaphoreType.DMA((steps,)),
        ],
        compiler_params=pltpu.CompilerParams(collective_id=0, has_side_effects=True),
    )(partial)


def swap_groups(parts):
    group = lax.broadcasted_iota(jnp.int32, parts[0].shape, 1) // ABLOCK
    even = group % 2 == 0
    low = group < 2
    p0, p1, p2, p3 = parts
    a0 = jnp.where(even, p0, pltpu.roll(p1, ABLOCK, 1))
    a1 = jnp.where(even, pltpu.roll(p0, LANES - ABLOCK, 1), p1)
    a2 = jnp.where(even, p2, pltpu.roll(p3, ABLOCK, 1))
    a3 = jnp.where(even, pltpu.roll(p2, LANES - ABLOCK, 1), p3)
    b0 = jnp.where(low, a0, pltpu.roll(a2, 2 * ABLOCK, 1))
    b2 = jnp.where(low, pltpu.roll(a0, 2 * ABLOCK, 1), a2)
    b1 = jnp.where(low, a1, pltpu.roll(a3, 2 * ABLOCK, 1))
    b3 = jnp.where(low, pltpu.roll(a1, 2 * ABLOCK, 1), a3)
    return [b0, b1, b2, b3]


def pack_kernel(block_cols, spill, target, sens, air, aloft, send, stage, sems):
    step = pl.program_id(0)
    last = pl.num_programs(0) - 1
    slot = step % 2

    def copy(row, place, col):
        return pltpu.make_async_copy(
            stage.at[place, col], send.at[target[row * block_cols + col]], sems.at[place, col]
        )

    def each(row, place, start):
        for col in range(block_cols):

            @pl.when(target[row * block_cols + col] < spill)
            def _():
                if start:
                    copy(row, place, col).start()
                else:
                    copy(row, place, col).wait()

    @pl.when(step >= 2)
    def _():
        each(step - 2, slot, False)

    level = air[0]
    fields = []
    for field in range(EXCHANGE_KINDS):
        flux = aloft[field].astype(jnp.float32) + sens[field] * level
        fields.append(flux)
    stacked = jnp.stack(fields, axis=0)
    rows = jnp.swapaxes(stacked, 0, 1)
    tall = ABLOCK // QUAD
    rows = rows.reshape(tall, QUAD, EXCHANGE_KINDS, rows.shape[-1])
    for group in range(block_cols // QUAD):
        parts = [
            rows[:, k, :, group * LANES : (group + 1) * LANES].reshape(tall * EXCHANGE_KINDS, LANES)
            for k in range(QUAD)
        ]
        swapped = swap_groups(parts)
        for j in range(QUAD):
            piece = swapped[j].reshape(tall, EXCHANGE_KINDS, LANES)
            flat = jnp.concatenate([piece[i] for i in range(tall)], axis=1)
            stage[slot, group * QUAD + j] = flat.astype(jnp.bfloat16)
    each(step, slot, True)

    @pl.when(step == last)
    def _():
        @pl.when(last >= 1)
        def _():
            each(step - 1, 1 - slot, False)

        each(step, slot, False)


def pack(advanced, aloft, sens, target, slots):
    levels, tile_rows, tile_cols = advanced.shape
    block_cols = tile_cols // ABLOCK
    return pl.pallas_call(
        functools.partial(pack_kernel, block_cols, slots),
        out_shape=jax.ShapeDtypeStruct((slots, EXCHANGE_KINDS, GAS_PATCH_TOTAL), jnp.bfloat16),
        grid_spec=pltpu.PrefetchScalarGridSpec(
            num_scalar_prefetch=2,
            grid=(tile_rows // ABLOCK,),
            in_specs=[
                pl.BlockSpec((1, ABLOCK, tile_cols), lambda i, *_: (levels - 1, i, 0)),
                pl.BlockSpec((EXCHANGE_KINDS, ABLOCK, tile_cols), lambda i, *_: (0, i, 0)),
            ],
            out_specs=pl.BlockSpec(memory_space=pl.ANY),
            scratch_shapes=[
                pltpu.VMEM((2, block_cols, EXCHANGE_KINDS, GAS_PATCH_TOTAL), jnp.bfloat16),
                pltpu.SemaphoreType.DMA((2, block_cols)),
            ],
        ),
        compiler_params=pltpu.CompilerParams(dimension_semantics=("arbitrary",)),
    )(target, sens, advanced, aloft)


def ocean_kernel(
    batch, arrival, total, incoming, warmth, forward, back, mix, flux_out, sst_out, back_out,
    taken, shaped, stage, in_sems, out_sems,
):
    step = pl.program_id(0)
    last = pl.num_programs(0) - 1
    slot = step % 2

    def fetch(at, place, start):
        for i in range(batch):
            place_of = at * batch + i

            @pl.when(place_of < total[0])
            def _():
                copy = pltpu.make_async_copy(
                    incoming.at[arrival[place_of]], taken.at[place, i], in_sems.at[place, i]
                )
                if start:
                    copy.start()
                else:
                    copy.wait()

    def put(at, place, start):
        for i in range(batch):
            place_of = at * batch + i

            @pl.when(place_of < total[0])
            def _():
                copy = pltpu.make_async_copy(
                    stage.at[place, i], back_out.at[arrival[place_of]], out_sems.at[place, i]
                )
                if start:
                    copy.start()
                else:
                    copy.wait()

    @pl.when(step == 0)
    def _():
        fetch(step, slot, True)

    @pl.when(step < last)
    def _():
        fetch(step + 1, 1 - slot, True)

    fetch(step, slot, False)

    @pl.when(step >= 2)
    def _():
        put(step - 2, slot, False)

    flat = batch * EXCHANGE_KINDS
    air = taken[slot].astype(jnp.float32).reshape(flat, GAS_PATCH_TOTAL)
    row_of = lax.broadcasted_iota(jnp.int32, (flat, 1), 0) // EXCHANGE_KINDS + step * batch
    held_wide = row_of < total[0]
    place = lax.broadcasted_iota(jnp.int32, (batch, 1), 0) + step * batch
    held = place < total[0]
    air_half = GAS_PATCH_TOTAL // 2
    sea_half = MARINE_PATCHES // 2
    for half in range(2):
        sea = slice(half * sea_half, (half + 1) * sea_half)
        part = air[:, half * air_half : (half + 1) * air_half].astype(jnp.bfloat16)
        grid_flux = jnp.dot(part, forward[...], preferred_element_type=jnp.float32)
        grid_flux = jnp.where(held_wide, grid_flux, 0.0).astype(jnp.bfloat16)
        flux_out[:, :, sea] = (
            grid_flux.astype(jnp.float32)
            .reshape(batch, EXCHANGE_KINDS, sea_half)
            .astype(jnp.bfloat16)
        )
        mixed = jnp.dot(mix[...], grid_flux, preferred_element_type=jnp.float32)
        warming = mixed[:batch] + mixed[batch:]
        renewed = jnp.where(held, warmth[:, sea] + warming, 0.0)
        sst_out[:, sea] = renewed
        upper = renewed.astype(jnp.bfloat16)
        lower = (renewed - upper.astype(jnp.float32)).astype(jnp.bfloat16)
        both = jnp.dot(
            jnp.concatenate([upper, lower], axis=0),
            back[...],
            preferred_element_type=jnp.float32,
        )
        home = (both[:batch] + both[batch:]) * (1.0 / 9.0)
        pieces = air_half // LANES
        for j in range(pieces):
            shaped[:, half * pieces + j, :] = home[:, j * LANES : (j + 1) * LANES]
    stage[slot] = shaped[...].astype(jnp.bfloat16)
    put(step, slot, True)

    @pl.when(step == last)
    def _():
        @pl.when(last >= 1)
        def _():
            put(step - 1, 1 - slot, False)

        put(step, slot, False)


def ocean(incoming, warmth, arrival, total, forward, back, mix):
    slots = incoming.shape[0]
    portion = warmth.shape[0]
    batch = SLOTS_STEP
    tall = GAS_PATCH_TOTAL // LANES
    return pl.pallas_call(
        functools.partial(ocean_kernel, batch),
        out_shape=(
            jax.ShapeDtypeStruct((portion, EXCHANGE_KINDS, MARINE_PATCHES), jnp.bfloat16),
            jax.ShapeDtypeStruct((portion, MARINE_PATCHES), jnp.float32),
            jax.ShapeDtypeStruct((slots, tall, LANES), jnp.bfloat16),
        ),
        grid_spec=pltpu.PrefetchScalarGridSpec(
            num_scalar_prefetch=2,
            grid=(portion // batch,),
            in_specs=[
                pl.BlockSpec(memory_space=pl.ANY),
                pl.BlockSpec((batch, MARINE_PATCHES), lambda i, *_: (i, 0)),
                pl.BlockSpec(memory_space=pltpu.VMEM),
                pl.BlockSpec(memory_space=pltpu.VMEM),
                pl.BlockSpec(memory_space=pltpu.VMEM),
            ],
            out_specs=(
                pl.BlockSpec((batch, EXCHANGE_KINDS, MARINE_PATCHES), lambda i, *_: (i, 0, 0)),
                pl.BlockSpec((batch, MARINE_PATCHES), lambda i, *_: (i, 0)),
                pl.BlockSpec(memory_space=pl.ANY),
            ),
            scratch_shapes=[
                pltpu.VMEM((2, batch, EXCHANGE_KINDS, GAS_PATCH_TOTAL), jnp.bfloat16),
                pltpu.VMEM((batch, tall, LANES), jnp.float32),
                pltpu.VMEM((2, batch, tall, LANES), jnp.bfloat16),
                pltpu.SemaphoreType.DMA((2, batch)),
                pltpu.SemaphoreType.DMA((2, batch)),
            ],
        ),
        compiler_params=pltpu.CompilerParams(
            dimension_semantics=("arbitrary",), vmem_limit_bytes=48 * 1024 * 1024
        ),
    )(arrival, total, incoming, warmth, forward, back, mix)


def surface_kernel(block_cols, spill, target, home, land, wet, out, taken, merged, sems):
    step = pl.program_id(0)
    last = pl.num_programs(0) - 1
    slot = step % AHEAD

    def fetch(row, place, start):
        for col in range(block_cols):

            @pl.when(target[row * block_cols + col] < spill)
            def _():
                copy = pltpu.make_async_copy(
                    home.at[target[row * block_cols + col]],
                    taken.at[place, col],
                    sems.at[place, col],
                )
                if start:
                    copy.start()
                else:
                    copy.wait()

    @pl.when(step == 0)
    def _():
        for early in range(AHEAD - 1):

            @pl.when(early <= last)
            def _():
                fetch(early, early, True)

    later = step + AHEAD - 1

    @pl.when(later <= last)
    def _():
        fetch(later, later % AHEAD, True)

    fetch(step, slot, False)
    tall = ABLOCK // QUAD
    for group in range(block_cols // QUAD):
        parts = [taken[slot, group * QUAD + j].astype(jnp.float32) for j in range(QUAD)]
        lines = swap_groups(parts)
        for k in range(QUAD):
            merged[group, pl.ds(k, tall, stride=QUAD), :] = lines[k]
        span = slice(group * LANES, (group + 1) * LANES)
        out[:, span] = jnp.where(
            wet[0, :, span] > 0.0, merged[group], land[:, span].astype(jnp.float32)
        )


def surface(home, land, wet_lanes, target):
    tile_rows, tile_cols = land.shape
    block_cols = tile_cols // ABLOCK
    slots, tall, _ = home.shape
    return pl.pallas_call(
        functools.partial(surface_kernel, block_cols, slots),
        out_shape=jax.ShapeDtypeStruct((tile_rows, tile_cols), jnp.float32),
        grid_spec=pltpu.PrefetchScalarGridSpec(
            num_scalar_prefetch=1,
            grid=(tile_rows // ABLOCK,),
            in_specs=[
                pl.BlockSpec(memory_space=pl.ANY),
                pl.BlockSpec((ABLOCK, tile_cols), lambda i, *_: (i, 0)),
                pl.BlockSpec((1, 1, tile_cols), lambda i, *_: (i, 0, 0)),
            ],
            out_specs=pl.BlockSpec((ABLOCK, tile_cols), lambda i, *_: (i, 0)),
            scratch_shapes=[
                pltpu.VMEM((AHEAD, block_cols, tall, LANES), jnp.bfloat16),
                pltpu.VMEM((tile_cols // LANES, ABLOCK, LANES), jnp.float32),
                pltpu.SemaphoreType.DMA((AHEAD, block_cols)),
            ],
        ),
        compiler_params=pltpu.CompilerParams(dimension_semantics=("arbitrary",)),
    )(target, home, land, wet_lanes)


def body(
    gaseous_model,
    forcing_boundary,
    relaxation_strength_profile,
    bottom_exchange_aloft,
    exchange_bottom_sensitivity,
    terrain_skin_warmth,
    tile_processor_home,
    marine_place_warmth,
    warming_coefficient,
):
    rows_ay = lax.axis_size("ay")
    cols_ax = lax.axis_size("ax")
    processor_roster = rows_ay * cols_ax
    device_id = lax.axis_index("ay") * cols_ax + lax.axis_index("ax")
    _, tile_rows, tile_cols = gaseous_model.shape
    block_rows = tile_rows // ABLOCK
    block_cols = tile_cols // ABLOCK
    processor_portion = block_rows * block_cols
    capacity = 2 * processor_portion // processor_roster
    slots = processor_roster * capacity
    basis_rows = spectral_basis(GRID, lax.axis_index("ay") * tile_rows, tile_rows, KMAX)
    basis_cols = spectral_basis(GRID, lax.axis_index("ax") * tile_cols, tile_cols, KMAX)
    departure = forcing_boundary - gaseous_model
    along_cols = jnp.einsum("lyx,xn->lyn", departure, basis_cols, precision=highest_accuracy)
    partial_sum = jnp.einsum("ym,lyn->lmn", basis_rows, along_cols, precision=highest_accuracy)
    modes = basis_rows.shape[1]
    padding = ((0, 0), (0, -modes % 8), (0, -modes % LANES))
    summed = sum_everywhere(jnp.pad(partial_sum, padding), (("ay", rows_ay), ("ax", cols_ax)))
    coefficients = summed[:, :modes, :modes]

    def nudged(state, strength, summed_modes):
        rows_back = jnp.einsum("ym,lmn->lyn", basis_rows, summed_modes, precision=highest_accuracy)
        filtered = jnp.einsum("lyn,xn->lyx", rows_back, basis_cols, precision=highest_accuracy)
        return state + strength[:, None, None] * filtered

    bottom = nudged(gaseous_model[-1:], relaxation_strength_profile[-1:], coefficients[-1:])

    owners = tile_processor_home.reshape(processor_roster, processor_portion)
    own_owner = lax.dynamic_index_in_dim(owners, device_id, 0, keepdims=False)
    numbers = jnp.arange(processor_portion, dtype=jnp.int32)
    earlier = numbers[:, None] > numbers[None, :]
    matching = own_owner[:, None] == own_owner[None, :]
    own_within = jnp.sum(matching & earlier, axis=1, dtype=jnp.int32)
    is_wet = own_owner < processor_roster
    target = jnp.where(is_wet, own_owner * capacity + own_within, slots).astype(jnp.int32)
    counts = jnp.sum(owners == device_id, axis=1, dtype=jnp.int32)
    tiles = jnp.arange(processor_roster, dtype=jnp.int32)
    ends = jnp.sum(jnp.where(tiles[:, None] >= tiles[None, :], counts[None, :], 0), axis=1)
    passed = numbers[:, None] >= ends[None, :]
    tile_of = jnp.sum(passed, axis=1, dtype=jnp.int32)
    before = jnp.sum(jnp.where(passed, counts[None, :], 0), axis=1, dtype=jnp.int32)
    held_total = jnp.sum(counts, dtype=jnp.int32).reshape(1)
    arrival = jnp.where(numbers < held_total, tile_of * capacity + numbers - before, 0)
    arrival = arrival.astype(jnp.int32)

    table = intersection_table()
    half_table = table[: MARINE_TILE_EDGE // 2, : ABLOCK // 2]
    paired = half_table[:, None, :, None] * table[None, :, None, :]
    paired = paired.reshape(MARINE_PATCHES // 2, GAS_PATCH_TOTAL // 2)
    forward_matrix = (paired / 4.0).T.astype(jnp.bfloat16)
    return_matrix = paired.astype(jnp.bfloat16)
    row_block = jnp.arange(SLOTS_STEP * EXCHANGE_KINDS, dtype=jnp.int32) // EXCHANGE_KINDS
    same = row_block[None, :] == jnp.arange(SLOTS_STEP, dtype=jnp.int32)[:, None]
    weights = jnp.where(same, jnp.tile(warming_coefficient, SLOTS_STEP)[None, :], 0.0)
    upper = lax.reduce_precision(weights, 8, 7)
    mix = jnp.concatenate([upper, weights - upper]).astype(jnp.bfloat16)
    wet_lanes = jnp.repeat(is_wet.reshape(block_rows, 1, block_cols), ABLOCK, axis=2)

    outgoing = pack(bottom, bottom_exchange_aloft, exchange_bottom_sensitivity, target, slots)
    outgoing, coefficients = lax.optimization_barrier((outgoing, coefficients))
    advanced_condition = nudged(gaseous_model, relaxation_strength_profile, coefficients)
    incoming = lax.all_to_all(outgoing, ("ay", "ax"), split_axis=0, concat_axis=0, tiled=True)
    marine_exchange_mesh, renewed_marine_warmth, outgoing_back = ocean(
        incoming, marine_place_warmth, arrival, held_total, forward_matrix, return_matrix, mix
    )
    home_rows = lax.all_to_all(outgoing_back, ("ay", "ax"), split_axis=0, concat_axis=0, tiled=True)
    bottom_quantity = surface(
        home_rows, terrain_skin_warmth, wet_lanes.astype(jnp.float32), target
    )
    return (advanced_condition, marine_exchange_mesh, renewed_marine_warmth, bottom_quantity)


def solution(mesh):
    return jax.shard_map(
        body,
        mesh=mesh,
        in_specs=(
            P(None, "ay", "ax"),
            P(None, "ay", "ax"),
            P(),
            P(None, "ay", "ax"),
            P(),
            P("ay", "ax"),
            P(),
            P(("ay", "ax"), None),
            P(),
        ),
        out_specs=(
            P(None, "ay", "ax"),
            P(("ay", "ax"), None, None),
            P(("ay", "ax"), None),
            P("ay", "ax"),
        ),
        check_vma=False,
    )
```
